32 devices in a mesh: grp: 2 (over y), queue: 4 (over z), tp: 2 (over x), seq: 2 (over core).
Axes of the slice: x: 2, y: 2, z: 4, core: 2. Of those that a mesh axis runs over, the one named last changes fastest.
Arguments:
- query_input: bfloat16 [8, 512, 1280], P(('grp', 'queue'), 'seq', 'tp'), parts along dimension 0, may hold values from -256 to 256
- key_input: bfloat16 [8, 512, 1280], P(('grp', 'queue'), 'seq', 'tp'), parts along dimension 0, may hold values from -256 to 256
- value_input: bfloat16 [8, 512, 1280], P(('grp', 'queue'), 'seq', 'tp'), parts along dimension 0, may hold values from -6 to 6
- query_gain: float32 [1280], P('tp'), may hold values from 0.1 to 1.9
- key_gain: float32 [1280], P('tp'), may hold values from 0.1 to 1.9
- gate_table: float32 [64, 1280], P(None, 'tp'), may hold values from -5 to 5
- levels: int32 [8], P(('grp', 'queue')), parts along dimension 0, may hold values from 0 to 63
Outputs:
- rolled: bfloat16 [8, 512, 1280], P(('grp', 'queue'), 'seq', 'tp'), parts along dimension 0
The draws below stay inside these ranges and needn't reach their ends.
There are 2 independent parts, one for each index of `grp`. The reference program is written for one: setup_inputs(seed, part) draws one part's arguments, and reference() takes and returns one part's arrays. A program takes and returns all parts, laid end to end along the dimension named above; an argument that names none is the same for every part. Nothing has to cross between parts.
All inputs are finite; a program needn't handle non-finite values.
Results may differ from the reference program's by a relative error of at most 0.0015.
The reference program's roundings to bfloat16 on the way count: a program that leaves them out, or rounds other values in their place, can miss the bound.
Values may be sent and summed in bfloat16 or wider, within the bound.
No kernel may reach another device: no remote copies, remote signals or barrier semaphores. Data moves between devices by JAX's collectives and lax.ppermute only.
A program may use at most 64 MiB of HBM per device.

```python
import math
import jax
import jax.numpy as jnp
from jax import lax

DH = 128
HEADS = 10
D = 1280
GROUP = 512
NQ = 4
LEVELS = 64


def make_field(key, which):
    noise_key = jax.random.fold_in(key, which)
    first, second, third = jax.random.split(noise_key, 3)
    columns = jnp.arange(D, dtype=jnp.float32) / D
    spread = jax.random.uniform(second, (D,), dtype=jnp.float32)
    row_draw = jax.random.uniform(third, (NQ, GROUP, 1), dtype=jnp.float32)
    base = jnp.clip(jax.random.normal(first, (NQ, GROUP, D), dtype=jnp.float32), -4.0, 4.0)
    column_scale = 10.0 ** spread * jnp.sqrt(1.0 + 2.2 * columns)
    row_scale = 10.0 ** (0.5 * row_draw)
    scaled = base * column_scale
    return scaled * row_scale


def draw_query_input(key, part):
    general = make_field(key, 1)
    return general.astype(jnp.bfloat16)


def draw_key_input(key, part):
    general = make_field(key, 2)
    return general.astype(jnp.bfloat16)


def place_ends(entries, key, least, largest):
    shape = entries.shape
    index_at = [jax.random.randint(jax.random.fold_in(key, axis), (), 0, shape[axis]) for axis in range(len(shape))]
    entries = entries.at[tuple(index_at)].set(least)
    longest = shape.index(max(shape))
    index_at[longest] = (index_at[longest] + 1) % shape[longest]
    return entries.at[tuple(index_at)].set(largest)


def steps_of(key, shape, shards, low, high):
    level, own = 1.0, jax.random.fold_in(key, 6)
    for axis_at, shards_of in shards:
        heights = jnp.exp(jax.random.uniform(jax.random.fold_in(own, axis_at), (shards_of,), jnp.float32, low / len(shards), high / len(shards)))
        level = level * jnp.repeat(heights, shape[axis_at] // shards_of).reshape([-1 if axis == axis_at else 1 for axis in range(len(shape))])
    return level


def normal_values(stream_key, extent, deviation, bound, cuts=(), kind=jnp.bfloat16):
    drawn = jax.random.normal(stream_key, extent, jnp.float32) * deviation
    if len(cuts) > 0:
        drawn = steps_of(stream_key, extent, cuts, -0.22, 0.18) * drawn
    return jnp.clip(drawn, min=-bound, max=bound).astype(kind)


def setup_inputs(seed: int = 0, part: int = 0) -> dict:
    seeds = jax.random.split(jax.random.key(seed), 8)
    part_splits = jax.random.split(jax.random.fold_in(seeds[7], part), 8)
    return {
        "query_input": draw_query_input(jax.random.fold_in(jax.random.fold_in(seeds[7], part), 71), part),
        "key_input": draw_key_input(jax.random.fold_in(jax.random.fold_in(seeds[7], part), 71), part),
        "value_input": normal_values(part_splits[2], (NQ, GROUP, D), 1.0, 6.0, ((0, 4), (1, 2), (2, 2))),
        "query_gain": jnp.clip(1.0 + 0.18 * jax.random.normal(seeds[3], (D,), jnp.float32), 0.1, 1.9),
        "key_gain": jnp.clip(1.0 + 0.18 * jax.random.normal(seeds[4], (D,), jnp.float32), 0.1, 1.9),
        "gate_table": normal_values(seeds[5], (LEVELS, D), 1.0, 5.0, ((1, 2),), jnp.float32),
        "levels": place_ends(jax.random.randint(part_splits[6], (NQ,), 0, LEVELS), jax.random.fold_in(part_splits[6], 1), 0, LEVELS - 1).astype(jnp.int32),
    }


epsilon = 1e-06

def normalize(field, gain):
    widened = field.astype(jnp.float32)
    square = lax.optimization_barrier(jnp.sum(widened * widened, axis=-1, keepdims=True))
    return (widened * lax.rsqrt(square / D + epsilon) * gain).astype(jnp.bfloat16)

def attend_head(items):
    head_query, head_key, head_value = items
    inverse_root = 1.0 / math.sqrt(DH)
    scores = jnp.dot(head_query, head_key.T, preferred_element_type=jnp.float32) * inverse_root
    row_max = lax.optimization_barrier(jnp.max(scores, axis=-1, keepdims=True))
    weights = jnp.exp(scores - row_max)
    weight_sum = lax.optimization_barrier(jnp.sum(weights, axis=-1, keepdims=True))
    summed = jnp.dot(weights.astype(jnp.bfloat16), head_value, preferred_element_type=jnp.float32)
    return summed / weight_sum

def reference(query_input, key_input, value_input, query_gain, key_gain, gate_table, levels):
    query_normed = normalize(query_input, query_gain)
    key_normed = normalize(key_input, key_gain)
    results = []
    for group_index in range(NQ):
        beside_all = [other for other in (group_index - 1, group_index, group_index + 1) if 0 <= other < NQ]
        key_block = jnp.concatenate([key_normed[other] for other in beside_all], axis=0)
        value_block = jnp.concatenate([value_input[other] for other in beside_all], axis=0)
        key_rows = key_block.shape[0]
        queries = query_normed[group_index].reshape(GROUP, HEADS, DH).transpose(1, 0, 2)
        head_keys = key_block.reshape(key_rows, HEADS, DH).transpose(1, 0, 2)
        head_values = value_block.reshape(key_rows, HEADS, DH).transpose(1, 0, 2)
        heads_out = lax.map(attend_head, (queries, head_keys, head_values))
        attended = heads_out.transpose(1, 0, 2).reshape(GROUP, D)
        gate_row = gate_table[levels[group_index]]
        results.append((gate_row * attended).astype(jnp.bfloat16))
    gated = jnp.stack(results)
    return jnp.roll(gated, -1, axis=0)
```

```python
import functools
import math

import jax
import jax.numpy as jnp
from jax import lax
from jax.experimental import pallas as pl
from jax.experimental.pallas import tpu as pltpu
from jax.sharding import PartitionSpec as P

DH = 128
EPSILON = 1e-06
SCALE = 1.0 / (math.sqrt(DH) * math.log(2.0))
CHUNK_SHARE = (3, 2)

LIMIT = 8 << 20
VMEM = pl.BlockSpec(memory_space=pltpu.VMEM)
SMEM = pl.BlockSpec(memory_space=pltpu.SMEM)


def chunk_widths(heads):
    first = (heads * CHUNK_SHARE[0]) // sum(CHUNK_SHARE)
    return [w * DH for w in (first, heads - first) if w > 0]


def row_square_sums(ref):
    rows, width = ref.shape
    total = None
    for start in range(0, width, DH):
        wide = ref[:, start : start + DH].astype(jnp.float32)
        total = wide * wide if total is None else total + wide * wide
    return jnp.sum(total.T, axis=0, keepdims=True)


def squares_kernel(query_ref, key_ref, out_ref):
    out_ref[0:1, :] = row_square_sums(query_ref)
    out_ref[1:2, :] = row_square_sums(key_ref)


def squares(query, key):
    rows = query.shape[0]
    return pl.pallas_call(
        squares_kernel,
        out_shape=jax.ShapeDtypeStruct((2, rows), jnp.float32),
        in_specs=[VMEM, VMEM],
        out_specs=VMEM,
        name="squares",
        compiler_params=pltpu.CompilerParams(vmem_limit_bytes=LIMIT),
    )(query, key)


def normalize_kernel(full_width, query_ref, key_ref, own_ref, other_ref, qgain_ref, kgain_ref, qout_ref, *kout_refs):
    rows = query_ref.shape[0]
    total = own_ref[...] + other_ref[...] if other_ref is not None else own_ref[...]
    factor = lax.rsqrt(total / full_width + EPSILON)
    spread = [jnp.broadcast_to(factor[i : i + 1, :], (DH, rows)).T for i in range(2)]
    at = 0
    for kout_ref in kout_refs:
        for start in range(0, kout_ref.shape[1], DH):
            wide = key_ref[:, at : at + DH].astype(jnp.float32)
            kout_ref[:, start : start + DH] = (wide * spread[1] * kgain_ref[:, at : at + DH]).astype(jnp.bfloat16)
            at += DH
    for start in range(0, query_ref.shape[1], DH):
        wide = query_ref[:, start : start + DH].astype(jnp.float32)
        qout_ref[:, start : start + DH] = (wide * spread[0] * qgain_ref[:, start : start + DH]).astype(jnp.bfloat16)


def normalize(query, key, own, other, query_gain, key_gain, full_width, widths):
    rows, width = query.shape
    return pl.pallas_call(
        functools.partial(normalize_kernel, full_width),
        out_shape=[jax.ShapeDtypeStruct((rows, w), jnp.bfloat16) for w in [width] + widths],
        in_specs=[VMEM] * 6,
        out_specs=[VMEM] * (1 + len(widths)),
        name="normalize",
        compiler_params=pltpu.CompilerParams(vmem_limit_bytes=LIMIT),
    )(query, key, own, other, query_gain[None], key_gain[None])


def attend(column, query_ref, key_refs, value_refs, gate, out_ref):
    for start in range(0, out_ref.shape[1], DH):
        here = slice(start, start + DH)
        there = slice(column + start, column + start + DH)
        head_query = query_ref[:, there]
        scores = [
            lax.dot_general(
                head_query, key_ref[:, here], (((1,), (1,)), ((), ())), preferred_element_type=jnp.float32
            )
            for key_ref in key_refs
        ]
        row_max = jnp.max(functools.reduce(jnp.maximum, scores), axis=1, keepdims=True)
        shift = row_max * SCALE
        weights = [jnp.exp2(part * SCALE - shift) for part in scores]
        weight_sum = jnp.sum(functools.reduce(jnp.add, weights), axis=1, keepdims=True)
        summed = functools.reduce(
            jnp.add,
            [
                jnp.dot(part.astype(jnp.bfloat16), value_ref[:, there], preferred_element_type=jnp.float32)
                for part, value_ref in zip(weights, value_refs)
            ],
        )
        out_ref[:, here] = (gate[:, there] * (summed / weight_sum)).astype(jnp.bfloat16)


def attention_kernel(column, scalars_ref, query_ref, gate_ref, *refs):
    keys, values, out_ref = refs[0:6], refs[6:12], refs[12]
    gate = gate_ref[pl.ds(scalars_ref[1], 1), :]

    @pl.when(scalars_ref[0] == 1)
    def _():
        attend(column, query_ref, keys, values, gate, out_ref)

    @pl.when(scalars_ref[0] == 0)
    def _():
        attend(column, query_ref, keys[:4], values[:4], gate, out_ref)


def attention(column, scalars, query, gate_table, keys, values):
    rows, width = query.shape[0], keys[0].shape[1]
    count = 6 * rows * width * rows
    return pl.pallas_call(
        functools.partial(attention_kernel, column),
        out_shape=jax.ShapeDtypeStruct((rows, width), jnp.bfloat16),
        in_specs=[SMEM] + [VMEM] * 14,
        out_specs=VMEM,
        name="attention",
        compiler_params=pltpu.CompilerParams(vmem_limit_bytes=LIMIT),
        cost_estimate=pl.CostEstimate(flops=4 * count, bytes_accessed=26 * rows * width, transcendentals=count // DH),
    )(scalars, query, gate_table, *keys, *values)


def body(query_input, key_input, value_input, query_gain, key_gain, gate_table, levels):
    places, seq, tp = (lax.axis_size(name) for name in ("queue", "seq", "tp"))
    rows, width = query_input.shape[1:]
    widths = chunk_widths(width // DH)
    first_pairs = [(i, i ^ 1) for i in range(places)]
    second_pairs = []
    for i in range(places):
        for s in range(seq):
            to = (i, 1 - s) if i in (0, places - 1) else (((i - 1) ^ 1) + 1, s)
            second_pairs.append((i * seq + s, to[0] * seq + to[1]))
    swap_pairs = [(s, 1 - s) for s in range(seq)]
    roll_pairs = [(i, (i - 1) % places) for i in range(places)]

    first = lambda x: lax.ppermute(x, "queue", first_pairs)
    second = lambda x: lax.ppermute(x, ("queue", "seq"), second_pairs)
    swap = lambda x: lax.ppermute(x, "seq", swap_pairs)

    query, key, value = query_input[0], key_input[0], value_input[0]
    value_first, value_second = first(value), second(value)
    own = squares(query, key)
    if tp == 2:
        other = lax.ppermute(own, "tp", [(0, 1), (1, 0)])
    else:
        own, other = lax.psum(own, "tp"), jnp.zeros_like(own)
    query_normed, *keys_normed = normalize(query, key, own, other, query_gain, key_gain, width * tp, widths)
    keys_first, keys_second = [], []
    for part in keys_normed:
        keys_first.append(first(part))
        keys_second.append(second(part))
    value_swapped = swap(value)
    keys_swapped = [swap(part) for part in keys_normed]
    values = [value, value_swapped, value_first, swap(value_first), value_second, swap(value_second)]

    place = lax.axis_index("queue")
    inner = (place > 0) & (place < places - 1)
    scalars = jnp.stack([inner.astype(jnp.int32), levels[0]])
    outputs, column = [], 0
    for i, part in enumerate(keys_normed):
        keys = [part, keys_swapped[i], keys_first[i], swap(keys_first[i]), keys_second[i], swap(keys_second[i])]
        gated = attention(column, scalars, query_normed, gate_table, keys, values)
        outputs.append(lax.ppermute(gated, "queue", roll_pairs))
        column += widths[i]
    return jnp.concatenate(outputs, axis=1)[None]


def solution(mesh):
    spec = P(("grp", "queue"), "seq", "tp")
    in_specs = (spec, spec, spec, P("tp"), P("tp"), P(None, "tp"), P(("grp", "queue")))
    return jax.shard_map(body, mesh=mesh, in_specs=in_specs, out_specs=spec, check_vma=False)
```

```python
import functools
import math

import jax
import jax.numpy as jnp
from jax import lax
from jax.experimental import pallas as pl
from jax.experimental.pallas import tpu as pltpu
from jax.sharding import PartitionSpec as P


DH = 128
EPSILON = 1e-06
SCALE = 1.0 / (math.sqrt(DH) * math.log(2.0))
CHUNK_SHARE = (3, 2)

LIMIT = 8 << 20
VMEM = pl.BlockSpec(memory_space=pltpu.VMEM)
HBM = pl.BlockSpec(memory_space=pltpu.HBM)
COPY_PARTS = 4
SMEM = pl.BlockSpec(memory_space=pltpu.SMEM)


def chunk_widths(heads):
    first = (heads * CHUNK_SHARE[0]) // sum(CHUNK_SHARE)
    return [w * DH for w in (first, heads - first) if w > 0]


def row_square_sums(ref):
    _, width = ref.shape
    total = None
    for start in range(0, width, DH):
        wide = ref[:, start : start + DH].astype(jnp.float32)
        total = wide * wide if total is None else total + wide * wide
    return jnp.sum(total.T, axis=0, keepdims=True)


def load_kernel(parts, *refs):
    query_hbm, key_hbm, value_hbm, *small_hbm = refs[:6]
    query_ref, key_ref, square_ref, *others = refs[6:-1]
    small_refs, value_refs, sems = others[:3], others[3:], refs[-1]
    copies = []

    def copy(source, target):
        copies.append(pltpu.make_async_copy(source, target, sems.at[len(copies)]))

    step = query_hbm.shape[0] // parts
    for source, target in ((query_hbm, query_ref), (key_hbm, key_ref)):
        for part in range(parts):
            copy(source.at[pl.ds(part * step, step)], target.at[pl.ds(part * step, step)])
    for source, target in zip(small_hbm, small_refs):
        copy(source, target)
    column = 0
    for target in value_refs:
        copy(value_hbm.at[:, pl.ds(column, target.shape[1])], target)
        column += target.shape[1]
    for started in copies:
        started.start()
    for which, ref in enumerate((query_ref, key_ref)):
        for started in copies[which * parts : (which + 1) * parts]:
            started.wait()
        square_ref[which : which + 1, :] = row_square_sums(ref)
    for started in copies[2 * parts :]:
        started.wait()


def load(query, key, value, query_gain, key_gain, gate_table, widths):
    rows, width = query.shape
    whole = jax.ShapeDtypeStruct((rows, width), query.dtype)
    sources = (query, key, value, query_gain, key_gain, gate_table)
    shapes = [whole, whole, jax.ShapeDtypeStruct((2, rows), jnp.float32)]
    shapes += [jax.ShapeDtypeStruct(x.shape, x.dtype) for x in sources[3:]]
    shapes += [jax.ShapeDtypeStruct((rows, chunk), value.dtype) for chunk in widths]
    return pl.pallas_call(
        functools.partial(load_kernel, COPY_PARTS),
        out_shape=shapes,
        in_specs=[HBM] * 6,
        out_specs=[VMEM] * len(shapes),
        scratch_shapes=[pltpu.SemaphoreType.DMA((2 * COPY_PARTS + 3 + len(widths),))],
        name="load",
        compiler_params=pltpu.CompilerParams(vmem_limit_bytes=LIMIT),
    )(*(pltpu.with_memory_space_constraint(x, pltpu.HBM) for x in sources))


def apply_norm(ref, factor, gain_ref, out_ref):
    rows, width = ref.shape
    spread = jnp.broadcast_to(factor, (DH, rows)).T
    for start in range(0, width, DH):
        here = slice(start, start + DH)
        wide = ref[:, here].astype(jnp.float32)
        out_ref[:, here] = (wide * spread * gain_ref[here]).astype(jnp.bfloat16)


def normalize_kernel(full_width, query_ref, key_ref, own_ref, other_ref, qgain_ref, kgain_ref, qout_ref, kout_ref, factor_ref):
    factor = lax.rsqrt((own_ref[...] + other_ref[...]) / full_width + EPSILON)
    factor_ref[...] = factor[1:2, :]
    apply_norm(key_ref, factor[1:2, :], kgain_ref, kout_ref)
    apply_norm(query_ref, factor[0:1, :], qgain_ref, qout_ref)


def normalize(query, key, own, other, query_gain, key_gain, full_width):
    rows = query.shape[0]
    kept = jax.ShapeDtypeStruct(query.shape, jnp.bfloat16)
    return pl.pallas_call(
        functools.partial(normalize_kernel, full_width),
        out_shape=[kept, kept, jax.ShapeDtypeStruct((1, rows), jnp.float32)],
        in_specs=[VMEM] * 6,
        out_specs=[VMEM] * 3,
        name="normalize",
        compiler_params=pltpu.CompilerParams(vmem_limit_bytes=LIMIT),
    )(query, key, own, other, query_gain, key_gain)


def normalize_two_kernel(a_ref, b_ref, afactor_ref, bfactor_ref, gain_ref, aout_ref, bout_ref):
    apply_norm(a_ref, afactor_ref[...], gain_ref, aout_ref)
    apply_norm(b_ref, bfactor_ref[...], gain_ref, bout_ref)


def normalize_two(a, b, afactor, bfactor, gain):
    kept = jax.ShapeDtypeStruct(a.shape, jnp.bfloat16)
    return pl.pallas_call(
        normalize_two_kernel,
        out_shape=[kept, kept],
        in_specs=[VMEM] * 5,
        out_specs=[VMEM] * 2,
        name="normalize_two",
        compiler_params=pltpu.CompilerParams(vmem_limit_bytes=LIMIT),
    )(a, b, afactor, bfactor, gain)


def with_used_blocks(work):
    place = lax.axis_index("queue")
    inner = (place > 0) & (place < lax.axis_size("queue") - 1)

    @pl.when(inner)
    def _():
        work(6)

    @pl.when(jnp.logical_not(inner))
    def _():
        work(4)


def scores_kernel(column, query_ref, *refs):
    keys, values = refs[0:6], refs[6:8]
    weight_ref, sum_ref, own_ref = refs[8:]
    rows = query_ref.shape[0]

    def work(used):
        for head in range(weight_ref.shape[0]):
            here = slice(head * DH, (head + 1) * DH)
            there = slice(column + head * DH, column + (head + 1) * DH)
            head_query = query_ref[:, there]
            scores = [
                lax.dot_general(
                    head_query, key_ref[:, there], (((1,), (1,)), ((), ())), preferred_element_type=jnp.float32
                )
                for key_ref in keys[:used]
            ]
            row_max = jnp.max(functools.reduce(jnp.maximum, scores), axis=1, keepdims=True)
            shift = row_max * SCALE
            weights = [jnp.exp2(part * SCALE - shift) for part in scores]
            weight_sum = jnp.sum(functools.reduce(jnp.add, weights), axis=1, keepdims=True)
            sum_ref[:, here] = jnp.broadcast_to(weight_sum, (rows, DH))
            low = [part.astype(jnp.bfloat16) for part in weights]
            for block in range(2, used):
                weight_ref[head, :, (block - 2) * rows : (block - 1) * rows] = low[block]
            own_ref[:, here] = functools.reduce(
                jnp.add,
                [
                    jnp.dot(part, value_ref[:, here], preferred_element_type=jnp.float32)
                    for part, value_ref in zip(low, values)
                ],
            )

    with_used_blocks(work)


def scores(column, width, query, keys, values):
    rows = query.shape[0]
    count = 6 * rows * width * rows
    return pl.pallas_call(
        functools.partial(scores_kernel, column),
        out_shape=[
            jax.ShapeDtypeStruct((width // DH, rows, 4 * rows), jnp.bfloat16),
            jax.ShapeDtypeStruct((rows, width), jnp.float32),
            jax.ShapeDtypeStruct((rows, width), jnp.float32),
        ],
        in_specs=[VMEM] * 9,
        out_specs=[VMEM] * 3,
        name="scores",
        compiler_params=pltpu.CompilerParams(vmem_limit_bytes=LIMIT),
        cost_estimate=pl.CostEstimate(flops=3 * count, bytes_accessed=26 * rows * width, transcendentals=count // DH),
    )(query, *keys, *values)


def gather_kernel(column, level_ref, gate_ref, weight_ref, sum_ref, own_ref, *refs):
    values, out_ref = refs[0:4], refs[4]
    rows = out_ref.shape[0]
    gate = gate_ref[pl.ds(level_ref[0], 1), :]

    def work(used):
        for head in range(out_ref.shape[1] // DH):
            here = slice(head * DH, (head + 1) * DH)
            there = slice(column + head * DH, column + (head + 1) * DH)
            summed = own_ref[:, here]
            for block in range(used - 2):
                summed += jnp.dot(
                    weight_ref[head, :, block * rows : (block + 1) * rows],
                    values[block][:, here],
                    preferred_element_type=jnp.float32,
                )
            out_ref[:, here] = (gate[:, there] * (summed / sum_ref[:, here])).astype(jnp.bfloat16)

    with_used_blocks(work)


def gather(column, width, levels, gate_table, weights, sums, own, values):
    rows = own.shape[0]
    count = 4 * rows * width * rows
    return pl.pallas_call(
        functools.partial(gather_kernel, column),
        out_shape=jax.ShapeDtypeStruct((rows, width), jnp.bfloat16),
        in_specs=[SMEM] + [VMEM] * 8,
        out_specs=VMEM,
        name="gather",
        compiler_params=pltpu.CompilerParams(vmem_limit_bytes=LIMIT),
        cost_estimate=pl.CostEstimate(flops=2 * count, bytes_accessed=26 * rows * width, transcendentals=0),
    )(levels, gate_table, weights, sums, own, *values)


def body(query_input, key_input, value_input, query_gain, key_gain, gate_table, levels):
    places, seq, tp = (lax.axis_size(name) for name in ("queue", "seq", "tp"))
    _, width = query_input.shape[1:]
    widths = chunk_widths(width // DH)
    first_pairs = [(i, i ^ 1) for i in range(places)]
    second_pairs = []
    for i in range(places):
        for s in range(seq):
            to = (i, 1 - s) if i in (0, places - 1) else (((i - 1) ^ 1) + 1, s)
            second_pairs.append((i * seq + s, to[0] * seq + to[1]))
    swap_pairs = [(s, 1 - s) for s in range(seq)]
    roll_pairs = [(i, (i - 1) % places) for i in range(places)]

    first = lambda x: lax.ppermute(x, "queue", first_pairs)
    second = lambda x: lax.ppermute(x, ("queue", "seq"), second_pairs)
    swap = lambda x: lax.ppermute(x, "seq", swap_pairs)

    query, key, value = query_input[0], key_input[0], value_input[0]
    key_first, key_second = first(key), second(key)
    query, key, own, query_gain, key_gain, gate_table, *value_parts = load(
        query, key, value, query_gain, key_gain, gate_table, widths
    )
    if tp == 2:
        other = lax.ppermute(own, "tp", [(0, 1), (1, 0)])
    else:
        own, other = lax.psum(own, "tp"), jnp.zeros_like(own)
    query_normed, key_normed, factor = normalize(query, key, own, other, query_gain, key_gain, width * tp)
    factor_first, factor_second = first(factor), second(factor)
    key_first, key_second = normalize_two(key_first, key_second, factor_first, factor_second, key_gain)
    keys = [key_normed, swap(key_normed), key_first, swap(key_first), key_second, swap(key_second)]
    outputs, column = [], 0
    for part in value_parts:
        chunk = part.shape[1]
        part_first, part_second = first(part), second(part)
        weights, sums, own = scores(column, chunk, query_normed, keys, [part, swap(part)])
        beside = [part_first, swap(part_first), part_second, swap(part_second)]
        gated = gather(column, chunk, levels, gate_table, weights, sums, own, beside)
        outputs.append(lax.ppermute(gated, "queue", roll_pairs))
        column += chunk
    return jnp.concatenate(outputs, axis=1)[None]


def solution(mesh):
    spec = P(("grp", "queue"), "seq", "tp")
    in_specs = (spec, spec, spec, P("tp"), P("tp"), P(None, "tp"), P(("grp", "queue")))
    return jax.shard_map(body, mesh=mesh, in_specs=in_specs, out_specs=spec, check_vma=False)
```

```python
import functools
import math

import jax
import jax.numpy as jnp
from jax import lax
from jax.experimental import pallas as pl
from jax.experimental.pallas import tpu as pltpu
from jax.sharding import PartitionSpec as P


DH = 128
EPSILON = 1e-06
SCALE = 1.0 / (math.sqrt(DH) * math.log(2.0))
CHUNK_SHARE = (3, 2)

LIMIT = 8 << 20
VMEM = pl.BlockSpec(memory_space=pltpu.VMEM)
HBM = pl.BlockSpec(memory_space=pltpu.HBM)
ANY = pl.BlockSpec(memory_space=pl.ANY)
COPY_PARTS = 4
SMEM = pl.BlockSpec(memory_space=pltpu.SMEM)


def chunk_widths(heads):
    first = (heads * CHUNK_SHARE[0]) // sum(CHUNK_SHARE)
    return [w * DH for w in (first, heads - first) if w > 0]


def row_square_sums(ref):
    _, width = ref.shape
    total = None
    for start in range(0, width, DH):
        wide = ref[:, start : start + DH].astype(jnp.float32)
        total = wide * wide if total is None else total + wide * wide
    return jnp.sum(total.T, axis=0, keepdims=True)


def squares_kernel(query_hbm, key_hbm, query_ref, key_ref, out_ref, sems):
    copies = []
    for which, (source, target) in enumerate(((query_hbm, query_ref), (key_hbm, key_ref))):
        step = source.shape[0] // COPY_PARTS
        for part in range(COPY_PARTS):
            rows = pl.ds(part * step, step)
            copies.append(pltpu.make_async_copy(source.at[rows], target.at[rows], sems.at[which, part]))
    for copy in copies:
        copy.start()
    for which, ref in enumerate((query_ref, key_ref)):
        for copy in copies[which * COPY_PARTS : (which + 1) * COPY_PARTS]:
            copy.wait()
        out_ref[which : which + 1, :] = row_square_sums(ref)


def squares(query, key):
    rows, width = query.shape
    kept = jax.ShapeDtypeStruct((rows, width), query.dtype)
    return pl.pallas_call(
        squares_kernel,
        out_shape=[kept, kept, jax.ShapeDtypeStruct((2, rows), jnp.float32)],
        in_specs=[HBM, HBM],
        out_specs=[VMEM] * 3,
        scratch_shapes=[pltpu.SemaphoreType.DMA((2, COPY_PARTS))],
        name="squares",
        compiler_params=pltpu.CompilerParams(vmem_limit_bytes=LIMIT),
    )(*(pltpu.with_memory_space_constraint(x, pltpu.HBM) for x in (query, key)))


def load_kernel(value_hbm, qgain_hbm, kgain_hbm, gate_hbm, levels_hbm, *refs):
    qgain_ref, kgain_ref, gate_ref, *value_refs = refs[:-3]
    table, level, sems = refs[-3:]
    pairs = [(levels_hbm, level), (gate_hbm, table), (qgain_hbm, qgain_ref), (kgain_hbm, kgain_ref)]
    column = 0
    for target in value_refs:
        pairs.append((value_hbm.at[:, pl.ds(column, target.shape[1])], target))
        column += target.shape[1]
    copies = [pltpu.make_async_copy(*pair, sems.at[i]) for i, pair in enumerate(pairs)]
    for copy in copies:
        copy.start()
    for copy in copies:
        copy.wait()
    gate_ref[...] = table[pl.ds(level[0], 1), :]


def load(value, query_gain, key_gain, gate_table, levels, widths):
    rows, width = value.shape
    gain = jax.ShapeDtypeStruct(query_gain.shape, query_gain.dtype)
    shapes = [gain, gain, jax.ShapeDtypeStruct((1, width), gate_table.dtype)]
    shapes += [jax.ShapeDtypeStruct((rows, chunk), value.dtype) for chunk in widths]
    sources = (value, query_gain, key_gain, gate_table)
    return pl.pallas_call(
        load_kernel,
        out_shape=shapes,
        in_specs=[HBM] * 4 + [ANY],
        out_specs=[VMEM] * len(shapes),
        scratch_shapes=[
            pltpu.VMEM(gate_table.shape, gate_table.dtype),
            pltpu.SMEM(levels.shape, levels.dtype),
            pltpu.SemaphoreType.DMA((4 + len(widths),)),
        ],
        name="load",
        compiler_params=pltpu.CompilerParams(vmem_limit_bytes=LIMIT),
    )(*(pltpu.with_memory_space_constraint(x, pltpu.HBM) for x in sources), levels)


def apply_norm(ref, factor, gain_ref, out_ref):
    rows, width = ref.shape
    spread = jnp.broadcast_to(factor, (DH, rows)).T
    for start in range(0, width, DH):
        here = slice(start, start + DH)
        wide = ref[:, here].astype(jnp.float32)
        out_ref[:, here] = (wide * spread * gain_ref[here]).astype(jnp.bfloat16)


def normalize_kernel(full_width, query_ref, key_ref, own_ref, other_ref, qgain_ref, kgain_ref, qout_ref, kout_ref, factor_ref):
    factor = lax.rsqrt((own_ref[...] + other_ref[...]) / full_width + EPSILON)
    factor_ref[...] = factor[1:2, :]
    apply_norm(key_ref, factor[1:2, :], kgain_ref, kout_ref)
    apply_norm(query_ref, factor[0:1, :], qgain_ref, qout_ref)


def normalize(query, key, own, other, query_gain, key_gain, full_width):
    rows = query.shape[0]
    kept = jax.ShapeDtypeStruct(query.shape, jnp.bfloat16)
    return pl.pallas_call(
        functools.partial(normalize_kernel, full_width),
        out_shape=[kept, kept, jax.ShapeDtypeStruct((1, rows), jnp.float32)],
        in_specs=[VMEM] * 6,
        out_specs=[VMEM] * 3,
        name="normalize",
        compiler_params=pltpu.CompilerParams(vmem_limit_bytes=LIMIT),
    )(query, key, own, other, query_gain, key_gain)


def normalize_two_kernel(a_ref, b_ref, afactor_ref, bfactor_ref, gain_ref, aout_ref, bout_ref):
    apply_norm(a_ref, afactor_ref[...], gain_ref, aout_ref)
    apply_norm(b_ref, bfactor_ref[...], gain_ref, bout_ref)


def normalize_two(a, b, afactor, bfactor, gain):
    kept = jax.ShapeDtypeStruct(a.shape, jnp.bfloat16)
    return pl.pallas_call(
        normalize_two_kernel,
        out_shape=[kept, kept],
        in_specs=[VMEM] * 5,
        out_specs=[VMEM] * 2,
        name="normalize_two",
        compiler_params=pltpu.CompilerParams(vmem_limit_bytes=LIMIT),
    )(a, b, afactor, bfactor, gain)


def with_used_blocks(work):
    place = lax.axis_index("queue")
    inner = (place > 0) & (place < lax.axis_size("queue") - 1)

    @pl.when(inner)
    def _():
        work(6)

    @pl.when(jnp.logical_not(inner))
    def _():
        work(4)


def scores_kernel(column, query_ref, *refs):
    keys, values = refs[0:6], refs[6:8]
    weight_ref, sum_ref, own_ref = refs[8:]
    rows = query_ref.shape[0]

    def work(used):
        for head in range(weight_ref.shape[0]):
            here = slice(head * DH, (head + 1) * DH)
            there = slice(column + head * DH, column + (head + 1) * DH)
            head_query = query_ref[:, there]
            scores = [
                lax.dot_general(
                    head_query, key_ref[:, there], (((1,), (1,)), ((), ())), preferred_element_type=jnp.float32
                )
                for key_ref in keys[:used]
            ]
            row_max = jnp.max(functools.reduce(jnp.maximum, scores), axis=1, keepdims=True)
            shift = row_max * SCALE
            weights = [jnp.exp2(part * SCALE - shift) for part in scores]
            weight_sum = jnp.sum(functools.reduce(jnp.add, weights), axis=1, keepdims=True)
            sum_ref[:, here] = jnp.broadcast_to(weight_sum, (rows, DH))
            low = [part.astype(jnp.bfloat16) for part in weights]
            for block in range(2, used):
                weight_ref[head, :, (block - 2) * rows : (block - 1) * rows] = low[block]
            own_ref[:, here] = functools.reduce(
                jnp.add,
                [
                    jnp.dot(part, value_ref[:, here], preferred_element_type=jnp.float32)
                    for part, value_ref in zip(low, values)
                ],
            )

    with_used_blocks(work)


def scores(column, width, query, keys, values):
    rows = query.shape[0]
    count = 6 * rows * width * rows
    return pl.pallas_call(
        functools.partial(scores_kernel, column),
        out_shape=[
            jax.ShapeDtypeStruct((width // DH, rows, 4 * rows), jnp.bfloat16),
            jax.ShapeDtypeStruct((rows, width), jnp.float32),
            jax.ShapeDtypeStruct((rows, width), jnp.float32),
        ],
        in_specs=[VMEM] * 9,
        out_specs=[VMEM] * 3,
        name="scores",
        compiler_params=pltpu.CompilerParams(vmem_limit_bytes=LIMIT),
        cost_estimate=pl.CostEstimate(flops=3 * count, bytes_accessed=26 * rows * width, transcendentals=count // DH),
    )(query, *keys, *values)


def gather_kernel(column, gate_ref, weight_ref, sum_ref, own_ref, *refs):
    values, out_ref = refs[0:4], refs[4]
    rows = out_ref.shape[0]

    def work(used):
        for head in range(out_ref.shape[1] // DH):
            here = slice(head * DH, (head + 1) * DH)
            there = slice(column + head * DH, column + (head + 1) * DH)
            summed = own_ref[:, here]
            for block in range(used - 2):
                summed += jnp.dot(
                    weight_ref[head, :, block * rows : (block + 1) * rows],
                    values[block][:, here],
                    preferred_element_type=jnp.float32,
                )
            out_ref[:, here] = (gate_ref[:, there] * (summed / sum_ref[:, here])).astype(jnp.bfloat16)

    with_used_blocks(work)


def gather(column, width, gate, weights, sums, own, values):
    rows = own.shape[0]
    count = 4 * rows * width * rows
    return pl.pallas_call(
        functools.partial(gather_kernel, column),
        out_shape=jax.ShapeDtypeStruct((rows, width), jnp.bfloat16),
        in_specs=[VMEM] * 8,
        out_specs=VMEM,
        name="gather",
        compiler_params=pltpu.CompilerParams(vmem_limit_bytes=LIMIT),
        cost_estimate=pl.CostEstimate(flops=2 * count, bytes_accessed=26 * rows * width, transcendentals=0),
    )(gate, weights, sums, own, *values)


def put_kernel(column, part_ref, *refs):
    out_ref, sem = refs[-2:]
    copy = pltpu.make_async_copy(part_ref, out_ref.at[:, pl.ds(column, part_ref.shape[1])], sem)
    copy.start()
    copy.wait()


def put(part, column, whole, width):
    rows = part.shape[0]
    kept = [] if whole is None else [whole]
    return pl.pallas_call(
        functools.partial(put_kernel, column),
        out_shape=jax.ShapeDtypeStruct((rows, width), part.dtype),
        in_specs=[VMEM] + [HBM] * len(kept),
        out_specs=HBM,
        scratch_shapes=[pltpu.SemaphoreType.DMA],
        input_output_aliases={1: 0} if kept else {},
        name="put",
        compiler_params=pltpu.CompilerParams(vmem_limit_bytes=LIMIT),
    )(part, *kept)


def body(query_input, key_input, value_input, query_gain, key_gain, gate_table, levels):
    places, seq, tp = (lax.axis_size(name) for name in ("queue", "seq", "tp"))
    _, width = query_input.shape[1:]
    widths = chunk_widths(width // DH)
    first_pairs = [(i, i ^ 1) for i in range(places)]
    second_pairs = []
    for i in range(places):
        for s in range(seq):
            to = (i, 1 - s) if i in (0, places - 1) else (((i - 1) ^ 1) + 1, s)
            second_pairs.append((i * seq + s, to[0] * seq + to[1]))
    swap_pairs = [(s, 1 - s) for s in range(seq)]
    roll_pairs = [(i, (i - 1) % places) for i in range(places)]

    first = lambda x: lax.ppermute(x, "queue", first_pairs)
    second = lambda x: lax.ppermute(x, ("queue", "seq"), second_pairs)
    swap = lambda x: lax.ppermute(x, "seq", swap_pairs)

    query, key, value = query_input[0], key_input[0], value_input[0]
    key_first, key_second = first(key), second(key)
    query, key, own = squares(query, key)
    query_gain, key_gain, gate, *value_parts = load(value, query_gain, key_gain, gate_table, levels, widths)
    if tp == 2:
        other = lax.ppermute(own, "tp", [(0, 1), (1, 0)])
    else:
        own, other = lax.psum(own, "tp"), jnp.zeros_like(own)
    query_normed, key_normed, factor = normalize(query, key, own, other, query_gain, key_gain, width * tp)
    factor_first, factor_second = first(factor), second(factor)
    key_first, key_second = normalize_two(key_first, key_second, factor_first, factor_second, key_gain)
    keys = [key_normed, swap(key_normed), key_first, swap(key_first), key_second, swap(key_second)]
    outputs, column = [], 0
    for part in value_parts:
        chunk = part.shape[1]
        part_first, part_second = first(part), second(part)
        weights, sums, own = scores(column, chunk, query_normed, keys, [part, swap(part)])
        beside = [part_first, swap(part_first), part_second, swap(part_second)]
        gated = gather(column, chunk, gate, weights, sums, own, beside)
        outputs.append(lax.ppermute(gated, "queue", roll_pairs))
        column += chunk
    whole, column = None, 0
    for part in outputs:
        whole = put(part, column, whole, width)
        column += part.shape[1]
    return whole[None]


def solution(mesh):
    spec = P(("grp", "queue"), "seq", "tp")
    in_specs = (spec, spec, spec, P("tp"), P("tp"), P(None, "tp"), P(("grp", "queue")))
    return jax.shard_map(body, mesh=mesh, in_specs=in_specs, out_specs=spec, check_vma=False)
```

```python
import functools
import math

import jax
import jax.numpy as jnp
from jax import lax
from jax.experimental import pallas as pl
from jax.experimental.pallas import tpu as pltpu
from jax.sharding import PartitionSpec as P


DH = 128
EPSILON = 1e-06
SCALE = 1.0 / (math.sqrt(DH) * math.log(2.0))
CHUNK_SHARE = (3, 2)

LIMIT = 8 << 20
VMEM = pl.BlockSpec(memory_space=pltpu.VMEM)
HBM = pl.BlockSpec(memory_space=pltpu.HBM)
ANY = pl.BlockSpec(memory_space=pl.ANY)
COPY_PARTS = 4
SMEM = pl.BlockSpec(memory_space=pltpu.SMEM)


def chunk_widths(heads):
    first = (heads * CHUNK_SHARE[0]) // sum(CHUNK_SHARE)
    return [w * DH for w in (first, heads - first) if w > 0]


def row_square_sums(ref):
    _, width = ref.shape
    total = None
    for start in range(0, width, DH):
        wide = ref[:, start : start + DH].astype(jnp.float32)
        total = wide * wide if total is None else total + wide * wide
    return jnp.sum(total.T, axis=0, keepdims=True)


def squares_kernel(query_hbm, key_hbm, query_ref, key_ref, out_ref, sems):
    copies = []
    for which, (source, target) in enumerate(((query_hbm, query_ref), (key_hbm, key_ref))):
        step = source.shape[0] // COPY_PARTS
        for part in range(COPY_PARTS):
            rows = pl.ds(part * step, step)
            copies.append(pltpu.make_async_copy(source.at[rows], target.at[rows], sems.at[which, part]))
    for copy in copies:
        copy.start()
    for which, ref in enumerate((query_ref, key_ref)):
        for copy in copies[which * COPY_PARTS : (which + 1) * COPY_PARTS]:
            copy.wait()
        out_ref[which : which + 1, :] = row_square_sums(ref)


def squares(query, key):
    rows, width = query.shape
    kept = jax.ShapeDtypeStruct((rows, width), query.dtype)
    return pl.pallas_call(
        squares_kernel,
        out_shape=[kept, kept, jax.ShapeDtypeStruct((2, rows), jnp.float32)],
        in_specs=[HBM, HBM],
        out_specs=[VMEM] * 3,
        scratch_shapes=[pltpu.SemaphoreType.DMA((2, COPY_PARTS))],
        name="squares",
        compiler_params=pltpu.CompilerParams(vmem_limit_bytes=LIMIT),
    )(*(pltpu.with_memory_space_constraint(x, pltpu.HBM) for x in (query, key)))


def load_kernel(value_hbm, qgain_hbm, kgain_hbm, gate_hbm, levels_hbm, *refs):
    qgain_ref, kgain_ref, gate_ref, *value_refs = refs[:-3]
    table, level, sems = refs[-3:]
    pairs = [(levels_hbm, level), (gate_hbm, table), (qgain_hbm, qgain_ref), (kgain_hbm, kgain_ref)]
    column = 0
    for target in value_refs:
        pairs.append((value_hbm.at[:, pl.ds(column, target.shape[1])], target))
        column += target.shape[1]
    copies = [pltpu.make_async_copy(*pair, sems.at[i]) for i, pair in enumerate(pairs)]
    for copy in copies:
        copy.start()
    for copy in copies:
        copy.wait()
    gate_ref[...] = table[pl.ds(level[0], 1), :]


def load(value, query_gain, key_gain, gate_table, levels, widths):
    rows, width = value.shape
    gain = jax.ShapeDtypeStruct(query_gain.shape, query_gain.dtype)
    shapes = [gain, gain, jax.ShapeDtypeStruct((1, width), gate_table.dtype)]
    shapes += [jax.ShapeDtypeStruct((rows, chunk), value.dtype) for chunk in widths]
    sources = (value, query_gain, key_gain, gate_table)
    return pl.pallas_call(
        load_kernel,
        out_shape=shapes,
        in_specs=[HBM] * 4 + [ANY],
        out_specs=[VMEM] * len(shapes),
        scratch_shapes=[
            pltpu.VMEM(gate_table.shape, gate_table.dtype),
            pltpu.SMEM(levels.shape, levels.dtype),
            pltpu.SemaphoreType.DMA((4 + len(widths),)),
        ],
        name="load",
        compiler_params=pltpu.CompilerParams(vmem_limit_bytes=LIMIT),
    )(*(pltpu.with_memory_space_constraint(x, pltpu.HBM) for x in sources), levels)


def apply_norm(ref, factor, gain_ref, out_ref):
    rows, width = ref.shape
    spread = jnp.broadcast_to(factor, (DH, rows)).T
    for start in range(0, width, DH):
        here = slice(start, start + DH)
        wide = ref[:, here].astype(jnp.float32)
        out_ref[:, here] = (wide * spread * gain_ref[here]).astype(jnp.bfloat16)


def normalize_kernel(full_width, query_ref, key_ref, own_ref, other_ref, qgain_ref, kgain_ref, qout_ref, kout_ref, factor_ref):
    factor = lax.rsqrt((own_ref[...] + other_ref[...]) / full_width + EPSILON)
    factor_ref[...] = factor[1:2, :]
    apply_norm(key_ref, factor[1:2, :], kgain_ref, kout_ref)
    apply_norm(query_ref, factor[0:1, :], qgain_ref, qout_ref)


def normalize(query, key, own, other, query_gain, key_gain, full_width):
    rows = query.shape[0]
    kept = jax.ShapeDtypeStruct(query.shape, jnp.bfloat16)
    return pl.pallas_call(
        functools.partial(normalize_kernel, full_width),
        out_shape=[kept, kept, jax.ShapeDtypeStruct((1, rows), jnp.float32)],
        in_specs=[VMEM] * 6,
        out_specs=[VMEM] * 3,
        name="normalize",
        compiler_params=pltpu.CompilerParams(vmem_limit_bytes=LIMIT),
    )(query, key, own, other, query_gain, key_gain)


def normalize_two_kernel(a_ref, b_ref, afactor_ref, bfactor_ref, gain_ref, aout_ref, bout_ref):
    apply_norm(a_ref, afactor_ref[...], gain_ref, aout_ref)
    apply_norm(b_ref, bfactor_ref[...], gain_ref, bout_ref)


def normalize_two(a, b, afactor, bfactor, gain):
    kept = jax.ShapeDtypeStruct(a.shape, jnp.bfloat16)
    return pl.pallas_call(
        normalize_two_kernel,
        out_shape=[kept, kept],
        in_specs=[VMEM] * 5,
        out_specs=[VMEM] * 2,
        name="normalize_two",
        compiler_params=pltpu.CompilerParams(vmem_limit_bytes=LIMIT),
    )(a, b, afactor, bfactor, gain)


def with_used_blocks(work):
    place = lax.axis_index("queue")
    inner = (place > 0) & (place < lax.axis_size("queue") - 1)

    @pl.when(inner)
    def _():
        work(6)

    @pl.when(jnp.logical_not(inner))
    def _():
        work(4)


def scores_kernel(column, query_ref, *refs):
    keys, values = refs[0:6], refs[6:8]
    weight_ref, sum_ref, own_ref = refs[8:]
    rows = query_ref.shape[0]

    heads = weight_ref.shape[0]

    def score(head, used):
        there = slice(column + head * DH, column + (head + 1) * DH)
        head_query = query_ref[:, there]
        return [
            lax.dot_general(
                head_query, key_ref[:, there], (((1,), (1,)), ((), ())), preferred_element_type=jnp.float32
            )
            for key_ref in keys[:used]
        ]

    def work(used):
        later = score(0, used)
        for head in range(heads):
            here = slice(head * DH, (head + 1) * DH)
            now = later
            row_max = jnp.max(functools.reduce(jnp.maximum, now), axis=1, keepdims=True)
            if head + 1 < heads:
                later = score(head + 1, used)
            shift = row_max * SCALE
            total, own = None, None
            for block, part in enumerate(now):
                weights = jnp.exp2(part * SCALE - shift)
                total = weights if total is None else total + weights
                low = weights.astype(jnp.bfloat16)
                if block < 2:
                    product = jnp.dot(low, values[block][:, here], preferred_element_type=jnp.float32)
                    own = product if own is None else own + product
                else:
                    weight_ref[head, :, (block - 2) * rows : (block - 1) * rows] = low
            sum_ref[:, here] = jnp.broadcast_to(jnp.sum(total, axis=1, keepdims=True), (rows, DH))
            own_ref[:, here] = own

    with_used_blocks(work)


def scores(column, width, query, keys, values):
    rows = query.shape[0]
    count = 6 * rows * width * rows
    return pl.pallas_call(
        functools.partial(scores_kernel, column),
        out_shape=[
            jax.ShapeDtypeStruct((width // DH, rows, 4 * rows), jnp.bfloat16),
            jax.ShapeDtypeStruct((rows, width), jnp.float32),
            jax.ShapeDtypeStruct((rows, width), jnp.float32),
        ],
        in_specs=[VMEM] * 9,
        out_specs=[VMEM] * 3,
        name="scores",
        compiler_params=pltpu.CompilerParams(vmem_limit_bytes=LIMIT),
        cost_estimate=pl.CostEstimate(flops=3 * count, bytes_accessed=26 * rows * width, transcendentals=count // DH),
    )(query, *keys, *values)


def gather_kernel(column, gate_ref, weight_ref, sum_ref, own_ref, *refs):
    values, out_ref = refs[0:4], refs[4]
    rows = out_ref.shape[0]

    def work(used):
        for head in range(out_ref.shape[1] // DH):
            here = slice(head * DH, (head + 1) * DH)
            there = slice(column + head * DH, column + (head + 1) * DH)
            summed = own_ref[:, here]
            for block in range(used - 2):
                summed += jnp.dot(
                    weight_ref[head, :, block * rows : (block + 1) * rows],
                    values[block][:, here],
                    preferred_element_type=jnp.float32,
                )
            out_ref[:, here] = (gate_ref[:, there] * (summed / sum_ref[:, here])).astype(jnp.bfloat16)

    with_used_blocks(work)


def gather(column, width, gate, weights, sums, own, values):
    rows = own.shape[0]
    count = 4 * rows * width * rows
    return pl.pallas_call(
        functools.partial(gather_kernel, column),
        out_shape=jax.ShapeDtypeStruct((rows, width), jnp.bfloat16),
        in_specs=[VMEM] * 8,
        out_specs=VMEM,
        name="gather",
        compiler_params=pltpu.CompilerParams(vmem_limit_bytes=LIMIT),
        cost_estimate=pl.CostEstimate(flops=2 * count, bytes_accessed=26 * rows * width, transcendentals=0),
    )(gate, weights, sums, own, *values)


def put_kernel(column, part_ref, *refs):
    out_ref, sem = refs[-2:]
    copy = pltpu.make_async_copy(part_ref, out_ref.at[:, pl.ds(column, part_ref.shape[1])], sem)
    copy.start()
    copy.wait()


def put(part, column, whole, width):
    rows = part.shape[0]
    kept = [] if whole is None else [whole]
    return pl.pallas_call(
        functools.partial(put_kernel, column),
        out_shape=jax.ShapeDtypeStruct((rows, width), part.dtype),
        in_specs=[VMEM] + [HBM] * len(kept),
        out_specs=HBM,
        scratch_shapes=[pltpu.SemaphoreType.DMA],
        input_output_aliases={1: 0} if kept else {},
        name="put",
        compiler_params=pltpu.CompilerParams(vmem_limit_bytes=LIMIT),
    )(part, *kept)


def body(query_input, key_input, value_input, query_gain, key_gain, gate_table, levels):
    places, seq, tp = (lax.axis_size(name) for name in ("queue", "seq", "tp"))
    _, width = query_input.shape[1:]
    widths = chunk_widths(width // DH)
    first_pairs = [(i, i ^ 1) for i in range(places)]
    second_pairs = []
    for i in range(places):
        for s in range(seq):
            to = (i, 1 - s) if i in (0, places - 1) else (((i - 1) ^ 1) + 1, s)
            second_pairs.append((i * seq + s, to[0] * seq + to[1]))
    swap_pairs = [(s, 1 - s) for s in range(seq)]
    roll_pairs = [(i, (i - 1) % places) for i in range(places)]

    first = lambda x: lax.ppermute(x, "queue", first_pairs)
    second = lambda x: lax.ppermute(x, ("queue", "seq"), second_pairs)
    swap = lambda x: lax.ppermute(x, "seq", swap_pairs)

    query, key, value = query_input[0], key_input[0], value_input[0]
    key_first, key_second = first(key), second(key)
    query, key, own = squares(query, key)
    query_gain, key_gain, gate, *value_parts = load(value, query_gain, key_gain, gate_table, levels, widths)
    if tp == 2:
        other = lax.ppermute(own, "tp", [(0, 1), (1, 0)])
    else:
        own, other = lax.psum(own, "tp"), jnp.zeros_like(own)
    query_normed, key_normed, factor = normalize(query, key, own, other, query_gain, key_gain, width * tp)
    factor_first, factor_second = first(factor), second(factor)
    key_first, key_second = normalize_two(key_first, key_second, factor_first, factor_second, key_gain)
    keys = [key_normed, swap(key_normed), key_first, swap(key_first), key_second, swap(key_second)]
    outputs, column = [], 0
    for part in value_parts:
        chunk = part.shape[1]
        part_first, part_second = first(part), second(part)
        weights, sums, own = scores(column, chunk, query_normed, keys, [part, swap(part)])
        beside = [part_first, swap(part_first), part_second, swap(part_second)]
        gated = gather(column, chunk, gate, weights, sums, own, beside)
        outputs.append(lax.ppermute(gated, "queue", roll_pairs))
        column += chunk
    whole, column = None, 0
    for part in outputs:
        whole = put(part, column, whole, width)
        column += part.shape[1]
    return whole[None]


def solution(mesh):
    spec = P(("grp", "queue"), "seq", "tp")
    in_specs = (spec, spec, spec, P("tp"), P("tp"), P(None, "tp"), P(("grp", "queue")))
    return jax.shard_map(body, mesh=mesh, in_specs=in_specs, out_specs=spec, check_vma=False)
```

```python
import functools
import math

import jax
import jax.numpy as jnp
from jax import lax
from jax.experimental import pallas as pl
from jax.experimental.pallas import tpu as pltpu
from jax.sharding import PartitionSpec as P


DH = 128
EPSILON = 1e-06
SCALE = 1.0 / (math.sqrt(DH) * math.log(2.0))
CHUNK_SHARE = (3, 2)

LIMIT = 8 << 20
VMEM = pl.BlockSpec(memory_space=pltpu.VMEM)
HBM = pl.BlockSpec(memory_space=pltpu.HBM)
ANY = pl.BlockSpec(memory_space=pl.ANY)
COPY_PARTS = 4
SMEM = pl.BlockSpec(memory_space=pltpu.SMEM)


def chunk_widths(heads):
    first = (heads * CHUNK_SHARE[0]) // sum(CHUNK_SHARE)
    return [w * DH for w in (first, heads - first) if w > 0]


def row_square_sums(ref):
    _, width = ref.shape
    total = None
    for start in range(0, width, DH):
        wide = ref[:, start : start + DH].astype(jnp.float32)
        total = wide * wide if total is None else total + wide * wide
    return jnp.sum(total.T, axis=0, keepdims=True)


def squares_kernel(query_hbm, key_hbm, query_ref, key_ref, out_ref, sems):
    copies = []
    for which, (source, target) in enumerate(((query_hbm, query_ref), (key_hbm, key_ref))):
        step = source.shape[0] // COPY_PARTS
        for part in range(COPY_PARTS):
            rows = pl.ds(part * step, step)
            copies.append(pltpu.make_async_copy(source.at[rows], target.at[rows], sems.at[which, part]))
    for copy in copies:
        copy.start()
    for which, ref in enumerate((query_ref, key_ref)):
        for copy in copies[which * COPY_PARTS : (which + 1) * COPY_PARTS]:
            copy.wait()
        out_ref[which : which + 1, :] = row_square_sums(ref)


def squares(query, key):
    rows, width = query.shape
    kept = jax.ShapeDtypeStruct((rows, width), query.dtype)
    return pl.pallas_call(
        squares_kernel,
        out_shape=[kept, kept, jax.ShapeDtypeStruct((2, rows), jnp.float32)],
        in_specs=[HBM, HBM],
        out_specs=[VMEM] * 3,
        scratch_shapes=[pltpu.SemaphoreType.DMA((2, COPY_PARTS))],
        name="squares",
        compiler_params=pltpu.CompilerParams(vmem_limit_bytes=LIMIT),
    )(*(pltpu.with_memory_space_constraint(x, pltpu.HBM) for x in (query, key)))


def load_kernel(value_hbm, qgain_hbm, kgain_hbm, gate_hbm, levels_hbm, *refs):
    qgain_ref, kgain_ref, gate_ref, *value_refs = refs[:-3]
    table, level, sems = refs[-3:]
    pairs = [(levels_hbm, level), (gate_hbm, table), (qgain_hbm, qgain_ref), (kgain_hbm, kgain_ref)]
    column = 0
    for target in value_refs:
        pairs.append((value_hbm.at[:, pl.ds(column, target.shape[1])], target))
        column += target.shape[1]
    copies = [pltpu.make_async_copy(*pair, sems.at[i]) for i, pair in enumerate(pairs)]
    for copy in copies:
        copy.start()
    for copy in copies:
        copy.wait()
    gate_ref[...] = table[pl.ds(level[0], 1), :]


def load(value, query_gain, key_gain, gate_table, levels, widths):
    rows, width = value.shape
    gain = jax.ShapeDtypeStruct(query_gain.shape, query_gain.dtype)
    shapes = [gain, gain, jax.ShapeDtypeStruct((1, width), gate_table.dtype)]
    shapes += [jax.ShapeDtypeStruct((rows, chunk), value.dtype) for chunk in widths]
    sources = (value, query_gain, key_gain, gate_table)
    return pl.pallas_call(
        load_kernel,
        out_shape=shapes,
        in_specs=[HBM] * 4 + [ANY],
        out_specs=[VMEM] * len(shapes),
        scratch_shapes=[
            pltpu.VMEM(gate_table.shape, gate_table.dtype),
            pltpu.SMEM(levels.shape, levels.dtype),
            pltpu.SemaphoreType.DMA((4 + len(widths),)),
        ],
        name="load",
        compiler_params=pltpu.CompilerParams(vmem_limit_bytes=LIMIT),
    )(*(pltpu.with_memory_space_constraint(x, pltpu.HBM) for x in sources), levels)


def apply_norm(ref, factor, gain_ref, out_ref):
    rows, width = ref.shape
    spread = jnp.broadcast_to(factor, (DH, rows)).T
    for start in range(0, width, DH):
        here = slice(start, start + DH)
        wide = ref[:, here].astype(jnp.float32)
        out_ref[:, here] = (wide * spread * gain_ref[here]).astype(jnp.bfloat16)


def normalize_kernel(full_width, query_ref, key_ref, own_ref, other_ref, qgain_ref, kgain_ref, qout_ref, kout_ref):
    factor = lax.rsqrt((own_ref[...] + other_ref[...]) / full_width + EPSILON)
    apply_norm(key_ref, factor[1:2, :], kgain_ref, kout_ref)
    apply_norm(query_ref, factor[0:1, :], qgain_ref, qout_ref)


def normalize(query, key, own, other, query_gain, key_gain, full_width):
    kept = jax.ShapeDtypeStruct(query.shape, jnp.bfloat16)
    return pl.pallas_call(
        functools.partial(normalize_kernel, full_width),
        out_shape=[kept, kept],
        in_specs=[VMEM] * 6,
        out_specs=[VMEM] * 2,
        name="normalize",
        compiler_params=pltpu.CompilerParams(vmem_limit_bytes=LIMIT),
    )(query, key, own, other, query_gain, key_gain)


def normalize_two_kernel(full_width, a_ref, b_ref, atotal_ref, btotal_ref, gain_ref, aout_ref, bout_ref):
    for ref, total_ref, out_ref in ((a_ref, atotal_ref, aout_ref), (b_ref, btotal_ref, bout_ref)):
        apply_norm(ref, lax.rsqrt(total_ref[...] / full_width + EPSILON), gain_ref, out_ref)


def normalize_two(a, b, atotal, btotal, gain, full_width):
    kept = jax.ShapeDtypeStruct(a.shape, jnp.bfloat16)
    return pl.pallas_call(
        functools.partial(normalize_two_kernel, full_width),
        out_shape=[kept, kept],
        in_specs=[VMEM] * 5,
        out_specs=[VMEM] * 2,
        name="normalize_two",
        compiler_params=pltpu.CompilerParams(vmem_limit_bytes=LIMIT),
    )(a, b, atotal, btotal, gain)


def with_used_blocks(work):
    place = lax.axis_index("queue")
    inner = (place > 0) & (place < lax.axis_size("queue") - 1)

    @pl.when(inner)
    def _():
        work(6)

    @pl.when(jnp.logical_not(inner))
    def _():
        work(4)


def scores_kernel(column, query_ref, *refs):
    keys, values = refs[0:6], refs[6:8]
    weight_ref, sum_ref, own_ref = refs[8:]
    rows = query_ref.shape[0]

    heads = weight_ref.shape[0]

    def score(head, used):
        there = slice(column + head * DH, column + (head + 1) * DH)
        head_query = query_ref[:, there]
        return [
            lax.dot_general(
                head_query, key_ref[:, there], (((1,), (1,)), ((), ())), preferred_element_type=jnp.float32
            )
            for key_ref in keys[:used]
        ]

    def work(used):
        later = score(0, used)
        for head in range(heads):
            here = slice(head * DH, (head + 1) * DH)
            now = later
            row_max = jnp.max(functools.reduce(jnp.maximum, now), axis=1, keepdims=True)
            if head + 1 < heads:
                later = score(head + 1, used)
            shift = row_max * SCALE
            total, own = None, None
            for block, part in enumerate(now):
                weights = jnp.exp2(part * SCALE - shift)
                total = weights if total is None else total + weights
                low = weights.astype(jnp.bfloat16)
                if block < 2:
                    product = jnp.dot(low, values[block][:, here], preferred_element_type=jnp.float32)
                    own = product if own is None else own + product
                else:
                    weight_ref[head, :, (block - 2) * rows : (block - 1) * rows] = low
            sum_ref[:, here] = jnp.broadcast_to(jnp.sum(total, axis=1, keepdims=True), (rows, DH))
            own_ref[:, here] = own

    with_used_blocks(work)


def scores(column, width, query, keys, values):
    rows = query.shape[0]
    count = 6 * rows * width * rows
    return pl.pallas_call(
        functools.partial(scores_kernel, column),
        out_shape=[
            jax.ShapeDtypeStruct((width // DH, rows, 4 * rows), jnp.bfloat16),
            jax.ShapeDtypeStruct((rows, width), jnp.float32),
            jax.ShapeDtypeStruct((rows, width), jnp.float32),
        ],
        in_specs=[VMEM] * 9,
        out_specs=[VMEM] * 3,
        name="scores",
        compiler_params=pltpu.CompilerParams(vmem_limit_bytes=LIMIT),
        cost_estimate=pl.CostEstimate(flops=3 * count, bytes_accessed=26 * rows * width, transcendentals=count // DH),
    )(query, *keys, *values)


def gather_kernel(column, gate_ref, weight_ref, sum_ref, own_ref, *refs):
    values, out_ref = refs[0:4], refs[4]
    rows = out_ref.shape[0]

    def work(used):
        for head in range(out_ref.shape[1] // DH):
            here = slice(head * DH, (head + 1) * DH)
            there = slice(column + head * DH, column + (head + 1) * DH)
            summed = own_ref[:, here]
            for block in range(used - 2):
                summed += jnp.dot(
                    weight_ref[head, :, block * rows : (block + 1) * rows],
                    values[block][:, here],
                    preferred_element_type=jnp.float32,
                )
            out_ref[:, here] = (gate_ref[:, there] * (summed / sum_ref[:, here])).astype(jnp.bfloat16)

    with_used_blocks(work)


def gather(column, width, gate, weights, sums, own, values):
    rows = own.shape[0]
    count = 4 * rows * width * rows
    return pl.pallas_call(
        functools.partial(gather_kernel, column),
        out_shape=jax.ShapeDtypeStruct((rows, width), jnp.bfloat16),
        in_specs=[VMEM] * 8,
        out_specs=VMEM,
        name="gather",
        compiler_params=pltpu.CompilerParams(vmem_limit_bytes=LIMIT),
        cost_estimate=pl.CostEstimate(flops=2 * count, bytes_accessed=26 * rows * width, transcendentals=0),
    )(gate, weights, sums, own, *values)


def put_kernel(column, part_ref, *refs):
    out_ref, sem = refs[-2:]
    copy = pltpu.make_async_copy(part_ref, out_ref.at[:, pl.ds(column, part_ref.shape[1])], sem)
    copy.start()
    copy.wait()


def put(part, column, whole, width):
    rows = part.shape[0]
    kept = [] if whole is None else [whole]
    return pl.pallas_call(
        functools.partial(put_kernel, column),
        out_shape=jax.ShapeDtypeStruct((rows, width), part.dtype),
        in_specs=[VMEM] + [HBM] * len(kept),
        out_specs=HBM,
        scratch_shapes=[pltpu.SemaphoreType.DMA],
        input_output_aliases={1: 0} if kept else {},
        name="put",
        compiler_params=pltpu.CompilerParams(vmem_limit_bytes=LIMIT),
    )(part, *kept)


def body(query_input, key_input, value_input, query_gain, key_gain, gate_table, levels):
    places, seq, tp = (lax.axis_size(name) for name in ("queue", "seq", "tp"))
    _, width = query_input.shape[1:]
    widths = chunk_widths(width // DH)
    first_pairs = [(i, i ^ 1) for i in range(places)]
    second_pairs = []
    for i in range(places):
        for s in range(seq):
            to = (i, 1 - s) if i in (0, places - 1) else (((i - 1) ^ 1) + 1, s)
            second_pairs.append((i * seq + s, to[0] * seq + to[1]))
    swap_pairs = [(s, 1 - s) for s in range(seq)]
    roll_pairs = [(i, (i - 1) % places) for i in range(places)]

    first = lambda x: lax.ppermute(x, "queue", first_pairs)
    second = lambda x: lax.ppermute(x, ("queue", "seq"), second_pairs)
    swap = lambda x: lax.ppermute(x, "seq", swap_pairs)

    query, key, value = query_input[0], key_input[0], value_input[0]
    key_first, key_second = first(key), second(key)
    query, key, own = squares(query, key)
    query_gain, key_gain, gate, *value_parts = load(value, query_gain, key_gain, gate_table, levels, widths)
    if tp == 2:
        other = lax.ppermute(own, "tp", [(0, 1), (1, 0)])
    else:
        own, other = lax.psum(own, "tp"), jnp.zeros_like(own)
    query_normed, key_normed = normalize(query, key, own, other, query_gain, key_gain, width * tp)
    total = own[1:2] + other[1:2]
    total_first, total_second = first(total), second(total)
    key_first, key_second = normalize_two(
        key_first, key_second, total_first, total_second, key_gain, width * tp
    )
    keys = [key_normed, swap(key_normed), key_first, swap(key_first), key_second, swap(key_second)]
    outputs, column = [], 0
    for part in value_parts:
        chunk = part.shape[1]
        part_first, part_second = first(part), second(part)
        weights, sums, own = scores(column, chunk, query_normed, keys, [part, swap(part)])
        beside = [part_first, swap(part_first), part_second, swap(part_second)]
        gated = gather(column, chunk, gate, weights, sums, own, beside)
        outputs.append(lax.ppermute(gated, "queue", roll_pairs))
        column += chunk
    whole, column = None, 0
    for part in outputs:
        whole = put(part, column, whole, width)
        column += part.shape[1]
    return whole[None]


def solution(mesh):
    spec = P(("grp", "queue"), "seq", "tp")
    in_specs = (spec, spec, spec, P("tp"), P("tp"), P(None, "tp"), P(("grp", "queue")))
    return jax.shard_map(body, mesh=mesh, in_specs=in_specs, out_specs=spec, check_vma=False)
```

```python
import functools
import math

import jax
import jax.numpy as jnp
from jax import lax
from jax.experimental import pallas as pl
from jax.experimental.pallas import tpu as pltpu
from jax.sharding import PartitionSpec as P


DH = 128
EPSILON = 1e-06
SCALE = 1.0 / (math.sqrt(DH) * math.log(2.0))
CHUNK_SHARE = (3, 2)

LIMIT = 16 << 20
VMEM = pl.BlockSpec(memory_space=pltpu.VMEM)
HBM = pl.BlockSpec(memory_space=pltpu.HBM)
ANY = pl.BlockSpec(memory_space=pl.ANY)
COPY_PARTS = 4
SMEM = pl.BlockSpec(memory_space=pltpu.SMEM)


def chunk_widths(heads):
    first = (heads * CHUNK_SHARE[0]) // sum(CHUNK_SHARE)
    return [w * DH for w in (first, heads - first) if w > 0]


def row_square_sums(ref):
    _, width = ref.shape
    total = None
    for start in range(0, width, DH):
        wide = ref[:, start : start + DH].astype(jnp.float32)
        total = wide * wide if total is None else total + wide * wide
    return jnp.sum(total.T, axis=0, keepdims=True)


def squares_kernel(query_hbm, key_hbm, query_ref, key_ref, out_ref, sems):
    copies = []
    for which, (source, target) in enumerate(((query_hbm, query_ref), (key_hbm, key_ref))):
        step = source.shape[0] // COPY_PARTS
        for part in range(COPY_PARTS):
            rows = pl.ds(part * step, step)
            copies.append(pltpu.make_async_copy(source.at[rows], target.at[rows], sems.at[which, part]))
    for copy in copies:
        copy.start()
    for which, ref in enumerate((query_ref, key_ref)):
        for copy in copies[which * COPY_PARTS : (which + 1) * COPY_PARTS]:
            copy.wait()
        out_ref[which : which + 1, :] = row_square_sums(ref)


def squares(query, key):
    rows, width = query.shape
    kept = jax.ShapeDtypeStruct((rows, width), query.dtype)
    return pl.pallas_call(
        squares_kernel,
        out_shape=[kept, kept, jax.ShapeDtypeStruct((2, rows), jnp.float32)],
        in_specs=[HBM, HBM],
        out_specs=[VMEM] * 3,
        scratch_shapes=[pltpu.SemaphoreType.DMA((2, COPY_PARTS))],
        name="squares",
        compiler_params=pltpu.CompilerParams(vmem_limit_bytes=LIMIT),
    )(*(pltpu.with_memory_space_constraint(x, pltpu.HBM) for x in (query, key)))


def load_kernel(value_hbm, qgain_hbm, kgain_hbm, gate_hbm, levels_hbm, *refs):
    qgain_ref, kgain_ref, gate_ref, *value_refs = refs[:-3]
    table, level, sems = refs[-3:]
    pairs = [(levels_hbm, level), (gate_hbm, table), (qgain_hbm, qgain_ref), (kgain_hbm, kgain_ref)]
    column = 0
    for target in value_refs:
        pairs.append((value_hbm.at[:, pl.ds(column, target.shape[1])], target))
        column += target.shape[1]
    copies = [pltpu.make_async_copy(*pair, sems.at[i]) for i, pair in enumerate(pairs)]
    for copy in copies:
        copy.start()
    for copy in copies:
        copy.wait()
    gate_ref[...] = table[pl.ds(level[0], 1), :]


def load(value, query_gain, key_gain, gate_table, levels, widths):
    rows, width = value.shape
    gain = jax.ShapeDtypeStruct(query_gain.shape, query_gain.dtype)
    shapes = [gain, gain, jax.ShapeDtypeStruct((1, width), gate_table.dtype)]
    shapes += [jax.ShapeDtypeStruct((rows, chunk), value.dtype) for chunk in widths]
    sources = (value, query_gain, key_gain, gate_table)
    return pl.pallas_call(
        load_kernel,
        out_shape=shapes,
        in_specs=[HBM] * 4 + [ANY],
        out_specs=[VMEM] * len(shapes),
        scratch_shapes=[
            pltpu.VMEM(gate_table.shape, gate_table.dtype),
            pltpu.SMEM(levels.shape, levels.dtype),
            pltpu.SemaphoreType.DMA((4 + len(widths),)),
        ],
        name="load",
        compiler_params=pltpu.CompilerParams(vmem_limit_bytes=LIMIT),
    )(*(pltpu.with_memory_space_constraint(x, pltpu.HBM) for x in sources), levels)


def apply_norm(ref, factor, gain_ref, out_ref):
    rows, width = ref.shape
    spread = jnp.broadcast_to(factor, (DH, rows)).T
    for start in range(0, width, DH):
        here = slice(start, start + DH)
        wide = ref[:, here].astype(jnp.float32)
        out_ref[:, here] = (wide * spread * gain_ref[here]).astype(jnp.bfloat16)


def normalize_kernel(full_width, query_ref, key_ref, own_ref, other_ref, qgain_ref, kgain_ref, qout_ref, kout_ref):
    factor = lax.rsqrt((own_ref[...] + other_ref[...]) / full_width + EPSILON)
    apply_norm(key_ref, factor[1:2, :], kgain_ref, kout_ref)
    apply_norm(query_ref, factor[0:1, :], qgain_ref, qout_ref)


def normalize(query, key, own, other, query_gain, key_gain, full_width):
    kept = jax.ShapeDtypeStruct(query.shape, jnp.bfloat16)
    return pl.pallas_call(
        functools.partial(normalize_kernel, full_width),
        out_shape=[kept, kept],
        in_specs=[VMEM] * 6,
        out_specs=[VMEM] * 2,
        name="normalize",
        compiler_params=pltpu.CompilerParams(vmem_limit_bytes=LIMIT),
    )(query, key, own, other, query_gain, key_gain)


def normalize_two_kernel(full_width, a_ref, b_ref, atotal_ref, btotal_ref, gain_ref, aout_ref, bout_ref):
    for ref, total_ref, out_ref in ((a_ref, atotal_ref, aout_ref), (b_ref, btotal_ref, bout_ref)):
        apply_norm(ref, lax.rsqrt(total_ref[...] / full_width + EPSILON), gain_ref, out_ref)


def normalize_two(a, b, atotal, btotal, gain, full_width):
    kept = jax.ShapeDtypeStruct(a.shape, jnp.bfloat16)
    return pl.pallas_call(
        functools.partial(normalize_two_kernel, full_width),
        out_shape=[kept, kept],
        in_specs=[VMEM] * 5,
        out_specs=[VMEM] * 2,
        name="normalize_two",
        compiler_params=pltpu.CompilerParams(vmem_limit_bytes=LIMIT),
    )(a, b, atotal, btotal, gain)


def with_used_blocks(work):
    place = lax.axis_index("queue")
    inner = (place > 0) & (place < lax.axis_size("queue") - 1)

    @pl.when(inner)
    def _():
        work(6)

    @pl.when(jnp.logical_not(inner))
    def _():
        work(4)


def scores_kernel(column, query_ref, *refs):
    keys, values = refs[0:6], refs[6:8]
    weight_ref, sum_ref, own_ref = refs[8:]
    rows = query_ref.shape[0]

    heads = weight_ref.shape[0]

    def score(head, used):
        there = slice(column + head * DH, column + (head + 1) * DH)
        head_query = query_ref[:, there]
        return [
            lax.dot_general(
                head_query, key_ref[:, there], (((1,), (1,)), ((), ())), preferred_element_type=jnp.float32
            )
            for key_ref in keys[:used]
        ]

    def work(used):
        later = score(0, used)
        for head in range(heads):
            here = slice(head * DH, (head + 1) * DH)
            now = later
            row_max = jnp.max(functools.reduce(jnp.maximum, now), axis=1, keepdims=True)
            if head + 1 < heads:
                later = score(head + 1, used)
            shift = row_max * SCALE
            total, own = None, None
            for block, part in enumerate(now):
                weights = jnp.exp2(part * SCALE - shift)
                total = weights if total is None else total + weights
                low = weights.astype(jnp.bfloat16)
                if block < 2:
                    product = jnp.dot(low, values[block][:, here], preferred_element_type=jnp.float32)
                    own = product if own is None else own + product
                else:
                    weight_ref[head, :, (block - 2) * rows : (block - 1) * rows] = low
            sum_ref[:, here] = jnp.broadcast_to(jnp.sum(total, axis=1, keepdims=True), (rows, DH))
            own_ref[:, here] = own

    with_used_blocks(work)


def scores(column, width, query, keys, values):
    rows = query.shape[0]
    count = 6 * rows * width * rows
    return pl.pallas_call(
        functools.partial(scores_kernel, column),
        out_shape=[
            jax.ShapeDtypeStruct((width // DH, rows, 4 * rows), jnp.bfloat16),
            jax.ShapeDtypeStruct((rows, width), jnp.float32),
            jax.ShapeDtypeStruct((rows, width), jnp.float32),
        ],
        in_specs=[VMEM] * 9,
        out_specs=[VMEM] * 3,
        name="scores",
        compiler_params=pltpu.CompilerParams(vmem_limit_bytes=LIMIT),
        cost_estimate=pl.CostEstimate(flops=3 * count, bytes_accessed=26 * rows * width, transcendentals=count // DH),
    )(query, *keys, *values)


def half_kernel(weight_ref, own_ref, first_ref, second_ref, out_ref):
    rows = out_ref.shape[0]

    def work(used):
        for head in range(out_ref.shape[1] // DH):
            here = slice(head * DH, (head + 1) * DH)
            summed = own_ref[:, here]
            for block, value_ref in ((0, first_ref), (2, second_ref)):
                if block < used - 2:
                    summed += jnp.dot(
                        weight_ref[head, :, block * rows : (block + 1) * rows],
                        value_ref[:, here],
                        preferred_element_type=jnp.float32,
                    )
            out_ref[:, here] = summed

    with_used_blocks(work)


def gather_kernel(column, gate_ref, weight_ref, sum_ref, half_ref, first_ref, second_ref, out_ref):
    rows = out_ref.shape[0]

    def work(used):
        for head in range(out_ref.shape[1] // DH):
            here = slice(head * DH, (head + 1) * DH)
            there = slice(column + head * DH, column + (head + 1) * DH)
            summed = half_ref[:, here]
            for block, value_ref in ((1, first_ref), (3, second_ref)):
                if block < used - 2:
                    summed += jnp.dot(
                        weight_ref[head, :, block * rows : (block + 1) * rows],
                        value_ref[:, here],
                        preferred_element_type=jnp.float32,
                    )
            out_ref[:, here] = (gate_ref[:, there] * (summed / sum_ref[:, here])).astype(jnp.bfloat16)

    with_used_blocks(work)


def half(weights, own, values):
    return pl.pallas_call(
        half_kernel,
        out_shape=jax.ShapeDtypeStruct(own.shape, own.dtype),
        in_specs=[VMEM] * 4,
        out_specs=VMEM,
        name="half",
        compiler_params=pltpu.CompilerParams(vmem_limit_bytes=LIMIT),
        cost_estimate=pl.CostEstimate(flops=4 * own.size * own.shape[0], bytes_accessed=6 * own.size, transcendentals=0),
    )(weights, own, *values)


def gather(column, gate, weights, sums, summed, values):
    rows, width = summed.shape
    return pl.pallas_call(
        functools.partial(gather_kernel, column),
        out_shape=jax.ShapeDtypeStruct((rows, width), jnp.bfloat16),
        in_specs=[VMEM] * 6,
        out_specs=VMEM,
        name="gather",
        compiler_params=pltpu.CompilerParams(vmem_limit_bytes=LIMIT),
        cost_estimate=pl.CostEstimate(flops=4 * rows * width * rows, bytes_accessed=6 * rows * width, transcendentals=0),
    )(gate, weights, sums, summed, *values)


def put_kernel(column, part_ref, *refs):
    out_ref, sems = refs[-2:]
    rows, width = part_ref.shape
    step = rows // COPY_PARTS
    copies = []
    for part in range(COPY_PARTS):
        here = pl.ds(part * step, step)
        copies.append(
            pltpu.make_async_copy(part_ref.at[here], out_ref.at[here, pl.ds(column, width)], sems.at[part])
        )
    for copy in copies:
        copy.start()
    for copy in copies:
        copy.wait()


def put(part, column, whole, width):
    rows = part.shape[0]
    kept = [] if whole is None else [whole]
    return pl.pallas_call(
        functools.partial(put_kernel, column),
        out_shape=jax.ShapeDtypeStruct((rows, width), part.dtype),
        in_specs=[VMEM] + [HBM] * len(kept),
        out_specs=HBM,
        scratch_shapes=[pltpu.SemaphoreType.DMA((COPY_PARTS,))],
        input_output_aliases={1: 0} if kept else {},
        name="put",
        compiler_params=pltpu.CompilerParams(vmem_limit_bytes=LIMIT),
    )(part, *kept)


def body(query_input, key_input, value_input, query_gain, key_gain, gate_table, levels):
    places, seq, tp = (lax.axis_size(name) for name in ("queue", "seq", "tp"))
    _, width = query_input.shape[1:]
    widths = chunk_widths(width // DH)
    first_pairs = [(i, i ^ 1) for i in range(places)]
    second_pairs = []
    for i in range(places):
        for s in range(seq):
            to = (i, 1 - s) if i in (0, places - 1) else (((i - 1) ^ 1) + 1, s)
            second_pairs.append((i * seq + s, to[0] * seq + to[1]))
    swap_pairs = [(s, 1 - s) for s in range(seq)]
    roll_pairs = [(i, (i - 1) % places) for i in range(places)]

    first = lambda x: lax.ppermute(x, "queue", first_pairs)
    second = lambda x: lax.ppermute(x, ("queue", "seq"), second_pairs)
    swap = lambda x: lax.ppermute(x, "seq", swap_pairs)

    query, key, value = query_input[0], key_input[0], value_input[0]
    key_first, key_second = first(key), second(key)
    query, key, own = squares(query, key)
    query_gain, key_gain, gate, *value_parts = load(value, query_gain, key_gain, gate_table, levels, widths)
    if tp == 2:
        other = lax.ppermute(own, "tp", [(0, 1), (1, 0)])
    else:
        own, other = lax.psum(own, "tp"), jnp.zeros_like(own)
    query_normed, key_normed = normalize(query, key, own, other, query_gain, key_gain, width * tp)
    total = own[1:2] + other[1:2]
    total_first, total_second = first(total), second(total)
    key_first, key_second = normalize_two(
        key_first, key_second, total_first, total_second, key_gain, width * tp
    )
    keys = [key_normed, swap(key_normed), key_first, swap(key_first), key_second, swap(key_second)]
    outputs, column = [], 0
    for part in value_parts:
        chunk = part.shape[1]
        part_first, part_second = first(part), second(part)
        weights, sums, own = scores(column, chunk, query_normed, keys, [part, swap(part)])
        summed = half(weights, own, [part_first, part_second])
        swapped = [swap(part_first), swap(part_second)]
        gated = gather(column, gate, weights, sums, summed, swapped)
        outputs.append(lax.ppermute(gated, "queue", roll_pairs))
        column += chunk
    whole, column = None, 0
    for part in outputs:
        whole = put(part, column, whole, width)
        column += part.shape[1]
    return whole[None]


def solution(mesh):
    spec = P(("grp", "queue"), "seq", "tp")
    in_specs = (spec, spec, spec, P("tp"), P("tp"), P(None, "tp"), P(("grp", "queue")))
    return jax.shard_map(body, mesh=mesh, in_specs=in_specs, out_specs=spec, check_vma=False)
```
